32 devices in a mesh: segment: 2 (over core), dp: 4 (over y, x), mp: 4 (over z).
Axes of the slice: x: 2, y: 2, z: 4, core: 2. Of those that a mesh axis runs over, the one named last changes fastest.
Arguments:
- token_ids: int32 [2, 256], replicated, may hold values from 0 to 32767
- table: bfloat16 [32768, 8192], P('dp', 'mp'), may hold values from -6 to 6
- w_up: bfloat16 [2, 8192, 32768], P('segment', 'mp', 'dp'), may hold values from -0.0625 to 0.0625
- w_down: bfloat16 [2, 32768, 8192], P('segment', 'dp', 'mp'), may hold values from -0.03125 to 0.03125
- cotangent: bfloat16 [2, 256, 8192], P(None, 'dp', 'mp'), may hold values from -6 to 6
Outputs:
- acts: bfloat16 [2, 2, 256, 8192], P('segment', None, 'dp', 'mp')
- grads: bfloat16 [2, 2, 256, 8192], P('segment', None, 'dp', 'mp')
The draws below stay inside these ranges and needn't reach their ends.
All inputs are finite; a program needn't handle non-finite values.
Results may differ from the reference program's by a relative error of at most 0.018.
Values may be sent and summed in bfloat16 or wider, within the bound.
A program may use at most 192 MiB of HBM per device.

```python
import math
import jax
import jax.numpy as jnp
import numpy as np
from jax import lax

D = 8192
FF = 32768
VOCAB = 32768
MICRO = 2
TOK_MB = 256
SEGMENTS = 2


def touch_ends(array, stream_key, smallest, top_value):
    dims = array.shape
    place = [jax.random.randint(jax.random.fold_in(stream_key, axis), (), 0, dims[axis]) for axis in range(len(dims))]
    array = array.at[tuple(place)].set(smallest)
    longest = dims.index(max(dims))
    place[longest] = (place[longest] + 1) % dims[longest]
    return array.at[tuple(place)].set(top_value)


def steps_of(key, shape, split, least, high):
    factor_of, own = 1.0, jax.random.fold_in(key, 6)
    for dim, shards_of in split:
        heights = jnp.exp(jax.random.uniform(jax.random.fold_in(own, dim), (shards_of,), jnp.float32, least / len(split), high / len(split)))
        factor_of = factor_of * jnp.repeat(heights, shape[dim] // shards_of).reshape([-1 if axis == dim else 1 for axis in range(len(shape))])
    return factor_of


def cumulative_ranks(amount, slope):
    loads = [(1 << 20) // math.isqrt(grade ** slope) + 1 for grade in range(1, amount + 1)]
    spread = 1 + sum(loads) // (1 << 30)
    return np.cumsum(np.array([max(1, weight // spread) for weight in loads]))


def ranked(rng, extent, number_of, slope):
    listing = cumulative_ranks(number_of, slope)
    pick = jax.random.randint(jax.random.fold_in(rng, 1), extent, 0, int(listing[number_of - 1]))
    standing = jnp.searchsorted(jnp.asarray(listing, jnp.int32), pick, side="right")
    return jax.random.permutation(jax.random.fold_in(rng, 2), number_of)[standing].astype(jnp.int32)


def centred(rng, shape, scale, most, shards=(), dtype=jnp.bfloat16):
    values = scale * jax.random.normal(rng, shape, jnp.float32)
    if shards:
        values = values * steps_of(rng, shape, shards, -0.22, 0.18)
    return jnp.clip(values, -most, most).astype(dtype)


def setup_inputs(seed: int = 0) -> dict:
    key_of = jax.random.split(jax.random.key(seed), 6)
    token_ids = touch_ends(ranked(key_of[0], (MICRO, TOK_MB), VOCAB, 2), jax.random.fold_in(key_of[0], 3), 0, VOCAB - 1).astype(jnp.int32)
    table = centred(key_of[1], (VOCAB, D), 1.0, 6.0, ((0, 4), (1, 4)))
    w_up = centred(key_of[2], (SEGMENTS, D, FF), D ** -0.5, 0.0625, ((0, 2), (1, 4), (2, 4)))
    w_down = centred(key_of[3], (SEGMENTS, FF, D), FF ** -0.5, 0.03125, ((0, 2), (1, 4), (2, 4)))
    cotangent = centred(key_of[4], (MICRO, TOK_MB, D), 1.0, 6.0, ((1, 4), (2, 4)))
    return dict(token_ids=token_ids, table=table, w_up=w_up, w_down=w_down, cotangent=cotangent)


root_coef = 0.7978845608028654


def gelu_value(value):
    return 0.5 * value * (1.0 + jnp.tanh(root_coef * (value + 0.044715 * value * value * value)))


def gelu_slope(value):
    inner = jnp.tanh(root_coef * (value + 0.044715 * value * value * value))
    return 0.5 * (1.0 + inner) + 0.5 * value * (1.0 - inner * inner) * root_coef * (1.0 + 0.134145 * value * value)


def section_forward(inputs, up_matrix, down_matrix):
    pre_act = jnp.dot(inputs, up_matrix, preferred_element_type=jnp.float32)
    hidden = gelu_value(pre_act).astype(jnp.bfloat16)
    mixed = jnp.dot(hidden, down_matrix, preferred_element_type=jnp.float32)
    return (inputs.astype(jnp.float32) + mixed).astype(jnp.bfloat16), pre_act


def section_backward(upstream, pre_act, up_matrix, down_matrix):
    back_hidden = lax.dot_general(upstream, down_matrix, (((1,), (1,)), ((), ())), preferred_element_type=jnp.float32)
    back_pre = (gelu_slope(pre_act) * back_hidden).astype(jnp.bfloat16)
    mixed = lax.dot_general(back_pre, up_matrix, (((1,), (1,)), ((), ())), preferred_element_type=jnp.float32)
    return (upstream.astype(jnp.float32) + mixed).astype(jnp.bfloat16)


def reference(token_ids, table, w_up, w_down, cotangent):
    first_outs, second_outs, first_grads, second_grads = [], [], [], []
    for micro_pos in range(MICRO):
        embedded = jnp.take(table, token_ids[micro_pos], axis=0)
        first_out, first_pre = section_forward(embedded, w_up[0], w_down[0])
        second_out, second_pre = section_forward(first_out, w_up[1], w_down[1])
        second_grad = section_backward(cotangent[micro_pos], second_pre, w_up[1], w_down[1])
        first_grad = section_backward(second_grad, first_pre, w_up[0], w_down[0])
        first_outs.append(first_out)
        second_outs.append(second_out)
        first_grads.append(first_grad)
        second_grads.append(second_grad)
    acts = jnp.stack([jnp.stack(first_outs), jnp.stack(second_outs)])
    grads = jnp.stack([jnp.stack(first_grads), jnp.stack(second_grads)])
    return acts, grads
```

```python
import functools

import jax
import jax.numpy as jnp
from jax import lax
from jax.experimental import pallas as pl
from jax.experimental.pallas import tpu as pltpu
from jax.sharding import PartitionSpec as P

CHUNK = 256
SKEW = 1
LAG = 2
BLOCK = 512
VMEM_BYTES = 67_043_328

root_coef = 0.7978845608028654


def gelu_value(value):
    return 0.5 * value * (1.0 + jnp.tanh(root_coef * (value + 0.044715 * value * value * value)))


def gelu_slope(value):
    inner = jnp.tanh(root_coef * (value + 0.044715 * value * value * value))
    return 0.5 * (1.0 + inner) + 0.5 * value * (1.0 - inner * inner) * root_coef * (
        1.0 + 0.134145 * value * value
    )


def relay_kernel(
    count_dp, count_mp, micros, chunks, width,
    emb_ref, cot_ref, up_ref, down_ref, acts_ref, grads_ref,
    xin, rs, ag, acc, up_buf, down_buf, stage, inbox, part, total,
    rs_send, rs_recv, ag_send, ag_recv, fin_send, fin_recv, x_send, x_recv, emb_send, emb_recv, w_sem,
):
    seg, d, p = lax.axis_index("segment"), lax.axis_index("dp"), lax.axis_index("mp")
    n = count_mp
    rows, model = xin.shape[1], xin.shape[2]
    local = rows // count_dp
    all_chunks = micros * chunks
    half = chunks * width
    block = min(BLOCK, model)
    own = pl.ds(pl.multiple_of(d * local, local), local)

    def rem_dp(value):
        return lax.rem(value, count_dp)

    def place(h):
        return p + h * (n - 1 - 2 * p)

    barrier = pltpu.get_barrier_semaphore()

    def greet(target):
        pl.semaphore_signal(barrier, inc=1, device_id=target, device_id_type=pl.DeviceIdType.MESH)

    for i in range(1, count_mp):
        greet((seg, d, lax.rem(p + i, count_mp)))
    for i in range(1, count_dp):
        greet((seg, rem_dp(d + i), p))
    for i in range(count_dp):
        greet((1 - seg, rem_dp(d + i), p))
    pl.semaphore_wait(barrier, count_mp - 1 + 2 * count_dp - 1)

    def remote(src, dst, send, recv, target):
        return pltpu.make_async_remote_copy(
            src_ref=src, dst_ref=dst, send_sem=send, recv_sem=recv,
            device_id=target, device_id_type=pl.DeviceIdType.MESH,
        )

    def rs_copy(i, h, k):
        nxt = lax.rem(p + 1 - 2 * h + n, n)
        return remote(rs.at[i, h, k], rs.at[i, h, k], rs_send.at[i, h, k], rs_recv.at[i, h, k], (seg, d, nxt))

    def ag_copy(i, h, k):
        nxt = lax.rem(p - 1 + 2 * h + n, n)
        return remote(ag.at[i, h, k], ag.at[i, h, k], ag_send.at[i, h, k], ag_recv.at[i, h, k], (seg, d, nxt))

    def fin_copy(e, src_rank, dst_rank):
        return remote(
            stage.at[pl.ds(pl.multiple_of(dst_rank * local, local), local)], inbox.at[e, src_rank],
            fin_send.at[e, dst_rank], fin_recv.at[e, src_rank], (seg, dst_rank, p),
        )

    def x_copy(src, i, src_rank, dst_rank, dst_seg):
        return remote(
            src, xin.at[i, pl.ds(pl.multiple_of(src_rank * local, local), local)],
            x_send.at[i, dst_rank], x_recv.at[i, src_rank], (dst_seg, dst_rank, p),
        )

    def emb_copy(m, src_rank, dst_rank):
        return remote(
            emb_ref.at[pl.ds(pl.multiple_of(dst_rank * local, local), local)], inbox.at[micros + m, src_rank],
            emb_send.at[dst_rank], emb_recv.at[m, src_rank], (0, dst_rank, p),
        )

    def wait_input(i, m):
        index = i * micros + m
        for j in range(count_dp):
            other = rem_dp(d + j)
            if i == 0 and j == 0:
                continue
            x_copy(acts_ref.at[0], index, other, other, seg).wait_recv()

    def finish_start(g, m):
        e = g * micros + m
        for j in range(count_dp):
            dst = rem_dp(d + j + 1)
            at = pl.ds(pl.multiple_of(dst * local, local), local)
            if j < count_dp - 1:
                stage[at] = acc[m, at].astype(stage.dtype)
                fin_copy(e, d, dst).start()

    def finish_end(g, m, out_ref):
        e = g * micros + m
        total[...] = xin[e, own].astype(jnp.float32) + acc[m, own]
        for j in range(1, count_dp):
            src = rem_dp(d + j)
            fin_copy(e, src, src).wait_recv()
            total[...] += inbox[e, src].astype(jnp.float32)
        out_ref[m] = total[...].astype(out_ref.dtype)
        if g == 0:
            for j in range(count_dp):
                x_copy(out_ref.at[m], micros + m, d, rem_dp(d + j), 1 - seg).start()
        for j in range(1, count_dp):
            fin_copy(e, d, rem_dp(d + j)).wait_send()

    def weight_copy(use, kind, h, k, slot):
        base = pl.multiple_of(h * half + lax.rem(k, chunks) * width, width)
        sem = w_sem.at[use, h, slot]
        if kind == "up":
            return pltpu.make_async_copy(up_ref.at[:, pl.ds(base, width)], up_buf.at[use * 4 + h * 2 + slot], sem)
        return pltpu.make_async_copy(down_ref.at[pl.ds(base, width), :], down_buf.at[h * 2 + slot], sem)

    def stream(i, a, first, second, epilogue, hooks):
        base = SKEW * (n - 1) if first is not None else 0
        steps = all_chunks + (SKEW * (n - 1) if first is not None else 0) + (SKEW * (n - 1) if second is not None else 0)

        def rs_index(h, t):
            return t - SKEW * place(h)

        def ag_index(h, t):
            return t - base - SKEW * (n - 1 - place(h))

        def valid(k):
            return (k >= 0) & (k < all_chunks)

        def prefetch(t, slot):
            def half_step(h, carry):
                if first is not None:
                    k = rs_index(h, t)

                    @pl.when(valid(k))
                    def _():
                        weight_copy(0, first, h, k, slot).start()

                if second is not None:
                    ka = ag_index(h, t)

                    @pl.when(valid(ka))
                    def _():
                        weight_copy(1, second, h, ka, slot).start()

                return carry

            lax.fori_loop(0, 2, half_step, 0)

        def forward(h, t):
            k, q = ag_index(h, t), place(h)

            @pl.when(valid(k))
            def _():
                @pl.when(q < n - 1)
                def _():
                    ag_copy(a, h, k).wait_recv()

                moves = (q > 0) if first is None else (q > 0) & (q < n - 1)

                @pl.when(moves)
                def _():
                    ag_copy(a, h, k).start()

        def reduce(h, t, slot):
            k, q = rs_index(h, t), place(h)

            @pl.when(valid(k))
            def _():
                m = lax.div(k, chunks)
                weight_copy(0, first, h, k, slot).wait()
                x = xin[i * micros + m]
                if first == "up":
                    part[...] = jnp.dot(x, up_buf[h * 2 + slot], preferred_element_type=jnp.float32)
                else:
                    part[...] = lax.dot_general(
                        x, down_buf[h * 2 + slot], (((1,), (1,)), ((), ())), preferred_element_type=jnp.float32
                    )

                @pl.when(q > 0)
                def _():
                    rs_copy(i, h, k).wait_recv()
                    part[...] += rs[i, h, k].astype(jnp.float32)

                @pl.when(q < n - 1)
                def _():
                    rs[i, h, k] = part[...].astype(rs.dtype)
                    rs_copy(i, h, k).start()

                @pl.when(q == n - 1)
                def _():
                    epilogue(h, k)
                    if second is not None:
                        ag_copy(a, h, k).start()

        def accumulate(h, t, slot):
            k = ag_index(h, t)

            @pl.when(valid(k))
            def _():
                m = lax.div(k, chunks)
                weight_copy(1, second, h, k, slot).wait()

                def columns(b, carry):
                    at = pl.ds(pl.multiple_of(b * block, block), block)
                    if second == "down":
                        acc[m, :, at] += jnp.dot(
                            ag[a, h, k], down_buf[h * 2 + slot, :, at], preferred_element_type=jnp.float32
                        )
                    else:
                        acc[m, :, at] += lax.dot_general(
                            ag[a, h, k], up_buf[4 + h * 2 + slot, at, :], (((1,), (1,)), ((), ())),
                            preferred_element_type=jnp.float32,
                        )
                    return carry

                lax.fori_loop(0, model // block, columns, 0)

        def step(t, carry):
            slot = lax.rem(t, 2)

            @pl.when(t + 1 < steps)
            def _():
                prefetch(t + 1, 1 - slot)

            for m in range(micros):

                @pl.when(t == m * chunks)
                def _():
                    if first is not None:
                        wait_input(i, m)
                    if second is not None:
                        acc[m] = jnp.zeros(acc.shape[1:], acc.dtype)

            def both(body):
                def run(h, inner):
                    body(h)
                    return inner

                lax.fori_loop(0, 2, run, 0)

            if second is not None:
                both(lambda h: forward(h, t))
            if first is not None:
                both(lambda h: reduce(h, t, slot))
            if second is not None:
                both(lambda h: accumulate(h, t, slot))
            for when, act in hooks:

                @pl.when(t == when)
                def _():
                    act()

            return carry

        prefetch(0, 0)
        lax.fori_loop(0, steps, step, 0)

    def ends(m, span):
        return (m + 1) * chunks - 1 + span * SKEW * (n - 1)

    def finish_hooks(g, span, out_ref):
        hooks = []
        for m in range(micros - 1):
            hooks.append((ends(m, span), functools.partial(finish_start, g, m)))
            hooks.append((ends(m, span) + LAG, functools.partial(finish_end, g, m, out_ref)))
        return hooks

    def send_forward(h, k):
        ag[0, h, k] = gelu_value(part[...]).astype(ag.dtype)
        rs[0, h, k] = part[...].astype(rs.dtype)

    def send_backward(h, k):
        ag[1, h, k] = (gelu_slope(rs[0, h, k].astype(jnp.float32)) * part[...]).astype(ag.dtype)

    def keep(h, k):
        rs[0, h, k] = part[...].astype(rs.dtype)

    def send_turn(h, k):
        pre = part[...]
        ag[0, h, k] = (gelu_slope(pre) * rs[0, h, k].astype(jnp.float32)).astype(ag.dtype)
        ag[1, h, k] = gelu_value(pre).astype(ag.dtype)

    last = micros - 1

    @pl.when(seg == 0)
    def _():
        for j in range(1, count_dp):
            emb_copy(0, d, rem_dp(d + j)).start()
        for m in range(micros):
            if m == 0:
                total[...] = emb_ref[own].astype(jnp.float32)
            else:
                total[...] = jnp.zeros(total.shape, total.dtype)
            for j in range(count_dp):
                src = rem_dp(d + j)
                if m == 0 and j == 0:
                    continue
                emb_copy(m, src, src).wait_recv()
                total[...] += inbox[micros + m, src].astype(jnp.float32)
            xin[m, own] = total[...].astype(xin.dtype)
            for j in range(1, count_dp):
                x_copy(xin.at[m, own], m, d, rem_dp(d + j), seg).start()
        stream(0, 0, "up", "down", send_forward, finish_hooks(0, 2, acts_ref))
        finish_start(0, last)
        finish_end(0, last, acts_ref)
        stream(1, 1, "down", "up", send_backward, finish_hooks(1, 2, grads_ref))
        finish_start(1, last)
        finish_end(1, last, grads_ref)
        for j in range(1, count_dp):
            emb_copy(0, d, rem_dp(d + j)).wait_send()

    @pl.when(seg == 1)
    def _():
        for j in range(count_dp):
            emb_copy(1, d, rem_dp(d + j)).start()
        for m in range(micros):
            xin[m, own] = cot_ref[m]
            for j in range(1, count_dp):
                x_copy(cot_ref.at[m], m, d, rem_dp(d + j), seg).start()
        stream(0, 0, "down", None, keep, [])
        stream(1, 0, "up", "up", send_turn, finish_hooks(0, 2, grads_ref))
        finish_start(0, last)
        stream(1, 1, None, "down", None, [(LAG, functools.partial(finish_end, 0, last, grads_ref))] + finish_hooks(1, 1, acts_ref))
        finish_start(1, last)
        finish_end(1, last, acts_ref)
        for j in range(count_dp):
            emb_copy(1, d, rem_dp(d + j)).wait_send()

    def drain(k, carry):
        for i in range(2):
            for h in range(2):

                @pl.when(place(h) < n - 1)
                def _():
                    rs_copy(i, h, k).wait_send()

                @pl.when(place(h) > 0)
                def _():
                    ag_copy(i, h, k).wait_send()

        return carry

    lax.fori_loop(0, all_chunks, drain, 0)
    for m in range(micros):
        for j in range(count_dp):
            if j > 0:
                x_copy(cot_ref.at[m], m, d, rem_dp(d + j), seg).wait_send()
            x_copy(cot_ref.at[m], micros + m, d, rem_dp(d + j), 1 - seg).wait_send()


def relay(emb, cotangent, w_up, w_down, count_dp, count_mp):
    micros, local, model = cotangent.shape
    rows = emb.shape[0]
    hidden = w_up.shape[1]
    chunks = max(1, hidden // 2 // CHUNK)
    width = hidden // 2 // chunks
    all_chunks = micros * chunks
    low, full = jnp.bfloat16, jnp.float32
    vmem = pl.BlockSpec(memory_space=pltpu.VMEM)
    hbm = pl.BlockSpec(memory_space=pl.ANY)
    dma = pltpu.SemaphoreType.DMA
    out = jax.ShapeDtypeStruct((micros, local, model), low)
    return pl.pallas_call(
        functools.partial(relay_kernel, count_dp, count_mp, micros, chunks, width),
        out_shape=(out, out),
        in_specs=[vmem, vmem, hbm, hbm],
        out_specs=(vmem, vmem),
        scratch_shapes=[
            pltpu.VMEM((2 * micros, rows, model), low),
            pltpu.VMEM((2, 2, all_chunks, rows, width), low),
            pltpu.VMEM((2, 2, all_chunks, rows, width), low),
            pltpu.VMEM((micros, rows, model), full),
            pltpu.VMEM((8, model, width), low),
            pltpu.VMEM((4, width, model), low),
            pltpu.VMEM((rows, model), low),
            pltpu.VMEM((2 * micros, count_dp, local, model), low),
            pltpu.VMEM((rows, width), full),
            pltpu.VMEM((local, model), full),
            dma((2, 2, all_chunks)),
            dma((2, 2, all_chunks)),
            dma((2, 2, all_chunks)),
            dma((2, 2, all_chunks)),
            dma((2 * micros, count_dp)),
            dma((2 * micros, count_dp)),
            dma((2 * micros, count_dp)),
            dma((2 * micros, count_dp)),
            dma((count_dp,)),
            dma((micros, count_dp)),
            dma((2, 2, 2)),
        ],
        compiler_params=pltpu.CompilerParams(
            collective_id=0, has_side_effects=True, vmem_limit_bytes=VMEM_BYTES
        ),
    )(emb, cotangent, w_up, w_down)


def on_device(token_ids, table, w_up, w_down, cotangent):
    table_rows = table.shape[0]
    ids = lax.dynamic_index_in_dim(token_ids, lax.axis_index("segment"), 0, keepdims=False)
    picked = ids - lax.axis_index("dp") * table_rows
    inside = (picked >= 0) & (picked < table_rows)
    fetched = jnp.take(table, jnp.clip(picked, 0, table_rows - 1), axis=0, mode="clip")
    emb = jnp.where(inside[:, None], fetched, jnp.zeros_like(fetched))
    acts, grads = relay(emb, cotangent, w_up[0], w_down[0], lax.axis_size("dp"), lax.axis_size("mp"))
    return acts[None], grads[None]


def solution(mesh):
    return jax.shard_map(
        on_device,
        mesh=mesh,
        in_specs=(
            P(),
            P("dp", "mp"),
            P("segment", "mp", "dp"),
            P("segment", "dp", "mp"),
            P(None, "dp", "mp"),
        ),
        out_specs=(P("segment", None, "dp", "mp"), P("segment", None, "dp", "mp")),
        check_vma=False,
    )
```

```python
import functools

import jax
import jax.numpy as jnp
from jax import lax
from jax.experimental import pallas as pl
from jax.experimental.pallas import tpu as pltpu
from jax.sharding import PartitionSpec as P

CHUNK = 256
SPLIT = 2
SKEW = 2
LAG = 2
BLOCK = 512
VMEM_BYTES = 67_043_328

root_coef = 0.7978845608028654


def gelu_value(value):
    return 0.5 * value * (1.0 + jnp.tanh(root_coef * (value + 0.044715 * value * value * value)))


def gelu_slope(value):
    inner = jnp.tanh(root_coef * (value + 0.044715 * value * value * value))
    return 0.5 * (1.0 + inner) + 0.5 * value * (1.0 - inner * inner) * root_coef * (
        1.0 + 0.134145 * value * value
    )


def relay_kernel(
    count_dp, count_mp, split, chunks, width,
    emb_ref, cot_ref, up_ref, down_ref, acts_ref, grads_ref,
    xin, rs, ag, acc, up_buf, down_buf, stage, inbox, part, total,
    rs_send, rs_recv, ag_send, ag_recv, fin_send, fin_recv, x_send, x_recv, emb_send, emb_recv, w_sem,
):
    seg, d, p = lax.axis_index("segment"), lax.axis_index("dp"), lax.axis_index("mp")
    n = count_mp
    rows, model = xin.shape[1], xin.shape[2]
    micros = acc.shape[0]
    lag = min(LAG, chunks - 1)
    local = rows // count_dp
    all_chunks = micros * chunks
    half = chunks * width
    block = min(BLOCK, model)
    own = pl.ds(pl.multiple_of(d * local, local), local)

    def rem_dp(value):
        return lax.rem(value, count_dp)

    def place(h):
        return p + h * (n - 1 - 2 * p)

    barrier = pltpu.get_barrier_semaphore()

    def greet(target):
        pl.semaphore_signal(barrier, inc=1, device_id=target, device_id_type=pl.DeviceIdType.MESH)

    for i in range(1, count_mp):
        greet((seg, d, lax.rem(p + i, count_mp)))
    for i in range(1, count_dp):
        greet((seg, rem_dp(d + i), p))
    for i in range(count_dp):
        greet((1 - seg, rem_dp(d + i), p))
    pl.semaphore_wait(barrier, count_mp - 1 + 2 * count_dp - 1)

    def remote(src, dst, send, recv, target):
        return pltpu.make_async_remote_copy(
            src_ref=src, dst_ref=dst, send_sem=send, recv_sem=recv,
            device_id=target, device_id_type=pl.DeviceIdType.MESH,
        )

    def rs_copy(i, h, k):
        nxt = lax.rem(p + 1 - 2 * h + n, n)
        return remote(rs.at[i, h, k], rs.at[i, h, k], rs_send.at[i, h, k], rs_recv.at[i, h, k], (seg, d, nxt))

    def ag_copy(i, h, k):
        nxt = lax.rem(p - 1 + 2 * h + n, n)
        return remote(ag.at[i, h, k], ag.at[i, h, k], ag_send.at[i, h, k], ag_recv.at[i, h, k], (seg, d, nxt))

    def fin_copy(e, src_rank, dst_rank):
        return remote(
            stage.at[pl.ds(pl.multiple_of(dst_rank * local, local), local)], inbox.at[e, src_rank],
            fin_send.at[e, dst_rank], fin_recv.at[e, src_rank], (seg, dst_rank, p),
        )

    def x_copy(src, i, src_rank, dst_rank, dst_seg):
        return remote(
            src, xin.at[i, pl.ds(pl.multiple_of(src_rank * local, local), local)],
            x_send.at[i, dst_rank], x_recv.at[i, src_rank], (dst_seg, dst_rank, p),
        )

    def emb_copy(m, src_rank, dst_rank):
        within = m % split
        return remote(
            emb_ref.at[pl.ds(pl.multiple_of(within * rows + dst_rank * local, local), local)],
            inbox.at[micros + m, src_rank],
            emb_send.at[within, dst_rank], emb_recv.at[m, src_rank], (0, dst_rank, p),
        )

    def embed_end(m):
        if m < split:
            total[...] = emb_ref[pl.ds(pl.multiple_of(m * rows + d * local, local), local)].astype(jnp.float32)
        else:
            total[...] = jnp.zeros(total.shape, total.dtype)
        for j in range(1 if m < split else 0, count_dp):
            src = rem_dp(d + j)
            emb_copy(m, src, src).wait_recv()
            total[...] += inbox[micros + m, src].astype(jnp.float32)
        xin[m, own] = total[...].astype(xin.dtype)
        for j in range(1, count_dp):
            x_copy(xin.at[m, own], m, d, rem_dp(d + j), seg).start()

    def wait_input(i, m):
        index = i * micros + m
        for j in range(count_dp):
            other = rem_dp(d + j)
            if i == 0 and j == 0:
                continue
            x_copy(acts_ref.at[0], index, other, other, seg).wait_recv()

    def finish_start(g, m):
        e = g * micros + m
        for j in range(count_dp):
            dst = rem_dp(d + j + 1)
            at = pl.ds(pl.multiple_of(dst * local, local), local)
            if j < count_dp - 1:
                stage[at] = acc[m, at].astype(stage.dtype)
                fin_copy(e, d, dst).start()

    def finish_end(g, m, out_ref):
        e = g * micros + m
        total[...] = xin[e, own].astype(jnp.float32) + acc[m, own]
        for j in range(1, count_dp):
            src = rem_dp(d + j)
            fin_copy(e, src, src).wait_recv()
            total[...] += inbox[e, src].astype(jnp.float32)
        out_ref[m] = total[...].astype(out_ref.dtype)
        if g == 0:
            for j in range(count_dp):
                x_copy(out_ref.at[m], micros + m, d, rem_dp(d + j), 1 - seg).start()
        for j in range(1, count_dp):
            fin_copy(e, d, rem_dp(d + j)).wait_send()

    def weight_copy(use, kind, h, k, slot):
        base = pl.multiple_of(h * half + lax.rem(k, chunks) * width, width)
        sem = w_sem.at[use, h, slot]
        if kind == "up":
            return pltpu.make_async_copy(up_ref.at[:, pl.ds(base, width)], up_buf.at[use * 4 + h * 2 + slot], sem)
        return pltpu.make_async_copy(down_ref.at[pl.ds(base, width), :], down_buf.at[h * 2 + slot], sem)

    def stream(i, a, first, second, epilogue, finish=None, hooks=()):
        base = SKEW * (n - 1) if first is not None else 0
        steps = all_chunks + (SKEW * (n - 1) if first is not None else 0) + (SKEW * (n - 1) if second is not None else 0)

        def rs_index(h, t):
            return t - SKEW * place(h)

        def ag_index(h, t):
            return t - base - SKEW * (n - 1 - place(h))

        def valid(k):
            return (k >= 0) & (k < all_chunks)

        def prefetch(t, slot):
            def half_step(h, carry):
                if first is not None:
                    k = rs_index(h, t)

                    @pl.when(valid(k))
                    def _():
                        weight_copy(0, first, h, k, slot).start()

                if second is not None:
                    ka = ag_index(h, t)

                    @pl.when(valid(ka))
                    def _():
                        weight_copy(1, second, h, ka, slot).start()

                return carry

            lax.fori_loop(0, 2, half_step, 0)

        def forward(h, t):
            k, q = ag_index(h, t), place(h)

            @pl.when(valid(k))
            def _():
                @pl.when(q < n - 1)
                def _():
                    ag_copy(a, h, k).wait_recv()

                moves = (q > 0) if first is None else (q > 0) & (q < n - 1)

                @pl.when(moves)
                def _():
                    ag_copy(a, h, k).start()

        def reduce(h, t, slot):
            k, q = rs_index(h, t), place(h)

            @pl.when(valid(k))
            def _():
                m = lax.div(k, chunks)
                weight_copy(0, first, h, k, slot).wait()
                x = xin[i * micros + m]
                if first == "up":
                    part[...] = jnp.dot(x, up_buf[h * 2 + slot], preferred_element_type=jnp.float32)
                else:
                    part[...] = lax.dot_general(
                        x, down_buf[h * 2 + slot], (((1,), (1,)), ((), ())), preferred_element_type=jnp.float32
                    )

                @pl.when(q > 0)
                def _():
                    rs_copy(i, h, k).wait_recv()
                    part[...] += rs[i, h, k].astype(jnp.float32)

                @pl.when(q < n - 1)
                def _():
                    rs[i, h, k] = part[...].astype(rs.dtype)
                    rs_copy(i, h, k).start()

                @pl.when(q == n - 1)
                def _():
                    epilogue(h, k)
                    if second is not None:
                        ag_copy(a, h, k).start()

        def accumulate(h, t, slot):
            k = ag_index(h, t)

            @pl.when(valid(k))
            def _():
                m = lax.div(k, chunks)
                weight_copy(1, second, h, k, slot).wait()

                def columns(b, carry):
                    at = pl.ds(pl.multiple_of(b * block, block), block)
                    if second == "down":
                        acc[m, :, at] += jnp.dot(
                            ag[a, h, k], down_buf[h * 2 + slot, :, at], preferred_element_type=jnp.float32
                        )
                    else:
                        acc[m, :, at] += lax.dot_general(
                            ag[a, h, k], up_buf[4 + h * 2 + slot, at, :], (((1,), (1,)), ((), ())),
                            preferred_element_type=jnp.float32,
                        )
                    return carry

                lax.fori_loop(0, model // block, columns, 0)

        def step(t, carry):
            slot = lax.rem(t, 2)

            @pl.when(t + 1 < steps)
            def _():
                prefetch(t + 1, 1 - slot)

            @pl.when((lax.rem(t, chunks) == 0) & (t < all_chunks))
            def _():
                m = lax.div(t, chunks)
                if first is not None:
                    wait_input(i, m)
                if second is not None:
                    acc[m] = jnp.zeros(acc.shape[1:], acc.dtype)

            def both(body):
                def run(h, inner):
                    body(h)
                    return inner

                lax.fori_loop(0, 2, run, 0)

            if second is not None:
                both(lambda h: forward(h, t))
            if first is not None:
                both(lambda h: reduce(h, t, slot))
            if second is not None:
                both(lambda h: accumulate(h, t, slot))
            if finish is not None:
                g, span, out_ref = finish
                past = t + 1 - span * SKEW * (n - 1)

                @pl.when((past >= chunks) & (past < all_chunks) & (lax.rem(past + chunks, chunks) == 0))
                def _():
                    finish_start(g, lax.div(past, chunks) - 1)

                late = past - lag

                @pl.when((late >= chunks) & (late < all_chunks) & (lax.rem(late + chunks, chunks) == 0))
                def _():
                    finish_end(g, lax.div(late, chunks) - 1, out_ref)

            for when, act in hooks:

                @pl.when(t == when)
                def _():
                    act()

            return carry

        prefetch(0, 0)
        lax.fori_loop(0, steps, step, 0)

    def send_forward(h, k):
        ag[0, h, k] = gelu_value(part[...]).astype(ag.dtype)
        rs[0, h, k] = part[...].astype(rs.dtype)

    def send_backward(h, k):
        ag[1, h, k] = (gelu_slope(rs[0, h, k].astype(jnp.float32)) * part[...]).astype(ag.dtype)

    def keep(h, k):
        rs[0, h, k] = part[...].astype(rs.dtype)

    def send_turn(h, k):
        pre = part[...]
        ag[0, h, k] = (gelu_slope(pre) * rs[0, h, k].astype(jnp.float32)).astype(ag.dtype)
        ag[1, h, k] = gelu_value(pre).astype(ag.dtype)

    last = micros - 1

    @pl.when(seg == 0)
    def _():
        for m in range(split):
            for j in range(1, count_dp):
                emb_copy(m, d, rem_dp(d + j)).start()
        embed_end(0)
        later = [((m - 1) * chunks + 1, functools.partial(embed_end, m)) for m in range(1, micros)]
        stream(0, 0, "up", "down", send_forward, (0, 2, acts_ref), later)
        finish_start(0, last)
        finish_end(0, last, acts_ref)
        stream(1, 1, "down", "up", send_backward, (1, 2, grads_ref))
        finish_start(1, last)
        finish_end(1, last, grads_ref)
        for m in range(split):
            for j in range(1, count_dp):
                emb_copy(m, d, rem_dp(d + j)).wait_send()

    @pl.when(seg == 1)
    def _():
        for m in range(split):
            for j in range(count_dp):
                emb_copy(split + m, d, rem_dp(d + j)).start()
        for m in range(micros):
            xin[m, own] = cot_ref[m]
            for j in range(1, count_dp):
                x_copy(cot_ref.at[m], m, d, rem_dp(d + j), seg).start()
        stream(0, 0, "down", None, keep)
        stream(1, 0, "up", "up", send_turn, (0, 2, grads_ref))
        finish_start(0, last)
        stream(1, 1, None, "down", None, (1, 1, acts_ref), [(lag, functools.partial(finish_end, 0, last, grads_ref))])
        finish_start(1, last)
        finish_end(1, last, acts_ref)
        for m in range(split):
            for j in range(count_dp):
                emb_copy(split + m, d, rem_dp(d + j)).wait_send()

    def drain(k, carry):
        for i in range(2):
            for h in range(2):

                @pl.when(place(h) < n - 1)
                def _():
                    rs_copy(i, h, k).wait_send()

                @pl.when(place(h) > 0)
                def _():
                    ag_copy(i, h, k).wait_send()

        return carry

    lax.fori_loop(0, all_chunks, drain, 0)
    for m in range(micros):
        for j in range(count_dp):
            if j > 0:
                x_copy(cot_ref.at[m], m, d, rem_dp(d + j), seg).wait_send()
            x_copy(cot_ref.at[m], micros + m, d, rem_dp(d + j), 1 - seg).wait_send()


def relay(emb, cotangent, w_up, w_down, split, count_dp, count_mp):
    micros, local, model = cotangent.shape
    rows = emb.shape[0] // split
    hidden = w_up.shape[1]
    chunks = max(1, hidden // 2 // CHUNK)
    width = hidden // 2 // chunks
    all_chunks = micros * chunks
    low, full = jnp.bfloat16, jnp.float32
    vmem = pl.BlockSpec(memory_space=pltpu.VMEM)
    hbm = pl.BlockSpec(memory_space=pl.ANY)
    dma = pltpu.SemaphoreType.DMA
    out = jax.ShapeDtypeStruct((micros, local, model), low)
    return pl.pallas_call(
        functools.partial(relay_kernel, count_dp, count_mp, split, chunks, width),
        out_shape=(out, out),
        in_specs=[vmem, vmem, hbm, hbm],
        out_specs=(vmem, vmem),
        scratch_shapes=[
            pltpu.VMEM((2 * micros, rows, model), low),
            pltpu.VMEM((2, 2, all_chunks, rows, width), low),
            pltpu.VMEM((2, 2, all_chunks, rows, width), low),
            pltpu.VMEM((micros, rows, model), full),
            pltpu.VMEM((8, model, width), low),
            pltpu.VMEM((4, width, model), low),
            pltpu.VMEM((rows, model), low),
            pltpu.VMEM((2 * micros, count_dp, local, model), low),
            pltpu.VMEM((rows, width), full),
            pltpu.VMEM((local, model), full),
            dma((2, 2, all_chunks)),
            dma((2, 2, all_chunks)),
            dma((2, 2, all_chunks)),
            dma((2, 2, all_chunks)),
            dma((2 * micros, count_dp)),
            dma((2 * micros, count_dp)),
            dma((2 * micros, count_dp)),
            dma((2 * micros, count_dp)),
            dma((split, count_dp)),
            dma((micros, count_dp)),
            dma((2, 2, 2)),
        ],
        compiler_params=pltpu.CompilerParams(
            collective_id=0, has_side_effects=True, vmem_limit_bytes=VMEM_BYTES
        ),
    )(emb, cotangent, w_up, w_down)


def on_device(token_ids, table, w_up, w_down, cotangent):
    table_rows = table.shape[0]
    count_dp, count_mp = lax.axis_size("dp"), lax.axis_size("mp")
    micros, local, model = cotangent.shape
    split = SPLIT if local % (16 * SPLIT) == 0 else 1
    ids = lax.dynamic_index_in_dim(token_ids, lax.axis_index("segment"), 0, keepdims=False)
    ids = ids.reshape(count_dp, split, local // split).transpose(1, 0, 2).reshape(-1)
    picked = ids - lax.axis_index("dp") * table_rows
    inside = (picked >= 0) & (picked < table_rows)
    fetched = jnp.take(table, jnp.clip(picked, 0, table_rows - 1), axis=0, mode="clip")
    emb = jnp.where(inside[:, None], fetched, jnp.zeros_like(fetched))
    groups = cotangent.reshape(micros * split, local // split, model)
    acts, grads = relay(emb, groups, w_up[0], w_down[0], split, count_dp, count_mp)
    return acts.reshape(cotangent.shape)[None], grads.reshape(cotangent.shape)[None]


def solution(mesh):
    return jax.shard_map(
        on_device,
        mesh=mesh,
        in_specs=(
            P(),
            P("dp", "mp"),
            P("segment", "mp", "dp"),
            P("segment", "dp", "mp"),
            P(None, "dp", "mp"),
        ),
        out_specs=(P("segment", None, "dp", "mp"), P("segment", None, "dp", "mp")),
        check_vma=False,
    )
```
